128 devices in a mesh: row: 16 (over z_hi, x, core), col: 8 (over z_lo, y).
Axes of the slice: x: 4, y: 4, z: 4 (z_hi: 2, z_lo: 2; z = z_hi * 2 + z_lo), core: 2. Of those that a mesh axis runs over, the one named last changes fastest.
Arguments:
- chol: float32 [12288, 640], P(('row', 'col')), may hold values from -6 to 6
- eps_occ: float32 [48], replicated, may hold values from -2 to -0.5
- eps_vir: float32 [256], replicated, may hold values from 0.3 to 3
Outputs:
- work: float32 [12288, 640], P(('row', 'col'))
- energies: float32 [2], replicated
The draws below stay inside these ranges and needn't reach their ends.
All inputs are finite; a program needn't handle non-finite values.
Results may differ from the reference program's by a relative error of at most 0.00013.
Values sent between devices are 32-bit elements; how exact they have to be, the bound alone decides.
No kernel may reach another device: no remote copies, remote signals or barrier semaphores. Data moves between devices by JAX's collectives and lax.ppermute only.
A program may use at most 128 MiB of HBM per device.

```python
import jax
import jax.numpy as jnp
from jax import lax

NO = 48
NV = 256
NAUX = 640
ITERS = 2
OV = 12288


def block_scale(own_key, shape, shards, least, top_value):
    loudness = 1.0
    for position, parts in shards:
        heights = jax.random.uniform(jax.random.fold_in(jax.random.fold_in(own_key, 6), position), (parts,), jnp.float32, least / len(shards), top_value / len(shards))
        loudness = loudness * jnp.repeat(jnp.exp(heights), shape[position] // parts).reshape((-1,) + (1,) * (len(shape) - 1 - position))
    return loudness


def normal_values(own_key, extent, scale, bound, split=(), kind=jnp.bfloat16):
    entries = jax.random.normal(own_key, extent, jnp.float32) * scale
    if len(split) > 0:
        entries = block_scale(own_key, extent, split, -0.22, 0.18) * entries
    return jnp.clip(entries, min=-bound, max=bound).astype(kind)


def setup_inputs(seed: int = 0) -> dict:
    splits = jax.random.split(jax.random.key(seed), 4)
    return {
        "chol": normal_values(splits[0], (OV, NAUX), 1.0, 6.0, ((0, 128),), jnp.float32),
        "eps_occ": jnp.clip(jax.random.uniform(splits[1], (NO,), jnp.float32, -2.0, -0.5), -2.0, -0.5),
        "eps_vir": jnp.clip(jax.random.uniform(splits[2], (NV,), jnp.float32, 0.3, 3.0), 0.3, 3.0),
    }


def reference(chol, eps_occ, eps_vir):
    total = NV * NO
    pair = (eps_vir[:, None] - eps_occ[None, :]).reshape(total)
    height = 8
    blocks = NV // height
    block_rows = height * NO
    work = jnp.zeros_like(chol)
    energies = []
    for step in range(ITERS):
        factor = chol + work

        def one_block(index):
            rows = lax.dynamic_slice_in_dim(factor, index * block_rows, block_rows, 0)
            row_pair = lax.dynamic_slice_in_dim(pair, index * block_rows, block_rows, 0)
            product = lax.dot_general(rows, factor, (((1,), (1,)), ((), ())), precision=lax.Precision.HIGHEST, preferred_element_type=jnp.float32)
            direct = product.reshape(height, NO, NV, NO)
            numerator = 2.0 * direct - jnp.transpose(direct, (0, 3, 2, 1))
            denominator = row_pair.reshape(height, NO, 1, 1) + pair.reshape(1, 1, NV, NO)
            tile = (-numerator / (jnp.float32(total) * denominator)).reshape(block_rows, total)
            return jnp.dot(tile, chol, precision=lax.Precision.HIGHEST, preferred_element_type=jnp.float32)

        work = lax.map(one_block, jnp.arange(blocks, dtype=jnp.int32)).reshape(total, NAUX)
        energies.append(jnp.sum(chol * work))
    return work, jnp.stack(energies) / jnp.float32(total)
```

```python
import functools

import jax
import jax.numpy as jnp
from jax import lax
from jax.experimental import pallas as pl
from jax.experimental.pallas import tpu as pltpu
from jax.sharding import Mesh
from jax.sharding import PartitionSpec as P

ITERS = 2
AXES = ("zh", "x", "c", "zl", "y")
NO = 48
NAUX = 640
TILES = NAUX // 128
GROUP = 4
VMEM = pl.BlockSpec(memory_space=pltpu.VMEM)
NT = (((1,), (1,)), ((), ()))


def x_step(v, shift, flip):
    pairs = []
    for zh in range(2):
        for x in range(4):
            for zl in range(2):
                to_zh, to_zl = (1 - zh, 1 - zl) if flip else (zh, zl)
                pairs.append(((zh * 4 + x) * 2 + zl, (to_zh * 4 + (x + shift) % 4) * 2 + to_zl))
    return lax.ppermute(v, ("zh", "x", "zl"), pairs)


def y_step(v, shift, flip):
    pairs = []
    for zl in range(2):
        for y in range(4):
            pairs.append((zl * 4 + y, (1 - zl if flip else zl) * 4 + (y + shift) % 4))
    return lax.ppermute(v, ("zl", "y"), pairs)


def core_swap(v):
    return lax.ppermute(v, "c", [(0, 1), (1, 0)])


def gather(own, steps):
    left = [s(own, 1, False) for s in steps]
    right = [s(own, -1, False) for s in steps]
    partner = [s(own, 0, True) for s in steps]
    sides = [jnp.concatenate(p, 1) for p in zip(left, right)]
    mine = [jnp.concatenate((own, p), 1) for p in partner]
    far = [s(v, 2, False) for s, v in zip(steps, mine)]
    far_sides = [s(v, 0, True) for s, v in zip(steps, sides)]
    return list(zip(mine, sides, far, far_sides))


def split(v):
    hi = v.astype(jnp.bfloat16)
    lo = (v - hi.astype(jnp.float32)).astype(jnp.bfloat16)
    return hi, lo


def occupied(k, i):
    return pl.ds(k * GROUP * NO + i, GROUP, stride=NO)


def interleave(refs, out_ref):
    count = GROUP * len(refs)

    for i in range(NO):
        for g, ref in enumerate(refs):
            at = i * count + g * GROUP
            for k in range(TILES):
                out_ref[at : at + GROUP, k * 128 : (k + 1) * 128] = ref[occupied(k, i), :]


def columns_kernel(*refs):
    parts, hi_ref, lo_ref, full = refs[:8], refs[8], refs[9], refs[10]
    interleave(parts, full)
    rows = 128

    def body(i, _):
        at = pl.ds(pl.multiple_of(i * rows, rows), rows)
        hi_ref[at, :], lo_ref[at, :] = split(full[at, :])
        return 0

    lax.fori_loop(0, full.shape[0] // rows, body, 0)


def flat(v):
    return v.reshape(-1, v.shape[2])


def split_columns(parts):
    parts = [flat(p) for p in parts]
    total = NO * GROUP * len(parts)
    shape = jax.ShapeDtypeStruct((total, NAUX), jnp.bfloat16)
    return pl.pallas_call(
        columns_kernel,
        out_shape=(shape, shape),
        in_specs=[VMEM] * len(parts),
        out_specs=(VMEM, VMEM),
        scratch_shapes=[pltpu.VMEM((total, NAUX), jnp.float32)],
        compiler_params=pltpu.CompilerParams(vmem_limit_bytes=48 << 20),
        name="split_columns",
    )(*parts)


def swap_chunks(v):
    lane = lax.broadcasted_iota(jnp.int32, v[0].shape, 1)
    low = lane < 64
    even = (lane // 32) % 2 == 0

    def halves(a, b):
        r = pltpu.roll(jnp.where(low, b, a), 64, 1)
        return jnp.where(low, a, r), jnp.where(low, r, b)

    def quarters(a, b):
        m = jnp.where(even, b, a)
        return (
            jnp.where(even, a, pltpu.roll(m, 32, 1)),
            jnp.where(even, pltpu.roll(m, 96, 1), b),
        )

    a0, a2 = halves(v[0], v[2])
    a1, a3 = halves(v[1], v[3])
    w0, w1 = quarters(a0, a1)
    w2, w3 = quarters(a2, a3)
    return w0, w1, w2, w3


def tile_kernel(count, scale, *refs):
    f_parts, c_parts = refs[:count], refs[count : 2 * count]
    (fhi, flo, chi, clo, row_pair, col_pair) = refs[2 * count : 2 * count + 6]
    outs = refs[2 * count + 6 : 3 * count + 6]
    energy = refs[3 * count + 6]
    rows_f, rhi, rlo, direct, thi, tlo = refs[3 * count + 7 :]
    na = GROUP * count
    height = NO * na
    width = fhi.shape[0]
    nb = width // NO
    per = 128 // nb
    blocks = NO // per
    tall = per * na

    interleave(f_parts, rows_f)
    for s in range(0, height, 128):
        rhi[s : s + 128, :], rlo[s : s + 128, :] = split(rows_f[s : s + 128, :])

    for n in range(0, width, 256):
        at = slice(n, n + 256)
        acc = lax.dot_general(rhi[...], fhi[at, :], NT, preferred_element_type=jnp.float32)
        acc += lax.dot_general(rhi[...], flo[at, :], NT, preferred_element_type=jnp.float32)
        acc += lax.dot_general(rlo[...], fhi[at, :], NT, preferred_element_type=jnp.float32)
        direct[:, at] = acc

    def strip(i, _):
        here = pl.ds(pl.multiple_of(i * tall, tall), tall)
        lanes = pl.ds(pl.multiple_of(i * 128, 128), 128)
        e_row = jnp.broadcast_to(row_pair[here, :], (tall, 128))
        for j in range(blocks):
            other = direct[j * tall : (j + 1) * tall, lanes]
            parts = [other[k * na : (k + 1) * na] for k in range(per)]
            swapped = jnp.concatenate(swap_chunks(parts), 0)
            at = slice(j * 128, (j + 1) * 128)
            value = 2.0 * direct[here, at] - swapped
            e_sum = e_row + col_pair[0:1, at]
            thi[here, at], tlo[here, at] = split(value / e_sum)
        return 0

    lax.fori_loop(0, blocks, strip, 0)

    for n in range(0, NAUX, 128):
        at = slice(n, n + 128)
        acc = jnp.dot(thi[...], chi[:, at], preferred_element_type=jnp.float32)
        acc += jnp.dot(thi[...], clo[:, at], preferred_element_type=jnp.float32)
        acc += jnp.dot(tlo[...], chi[:, at], preferred_element_type=jnp.float32)
        rows_f[:, at] = acc * scale

    total = jnp.zeros((GROUP, 128), jnp.float32)
    for i in range(NO):
        for g in range(count):
            at = i * na + g * GROUP
            for k in range(TILES):
                w = rows_f[at : at + GROUP, k * 128 : (k + 1) * 128]
                outs[g][occupied(k, i), :] = w
                total += w * c_parts[g][occupied(k, i), :]
    energy[...] = jnp.full(energy.shape, jnp.sum(total), jnp.float32)


def tile(f_parts, c_parts, f_split, c_split, row_pair, col_pair, total):
    count = len(f_parts)
    height = NO * GROUP * count
    width = f_split[0].shape[0]
    part = jax.ShapeDtypeStruct((TILES * NO * GROUP, 128), jnp.float32)
    out = pl.pallas_call(
        functools.partial(tile_kernel, count, -1.0 / total),
        out_shape=(part,) * count + (jax.ShapeDtypeStruct((8, 128), jnp.float32),),
        in_specs=[VMEM] * (2 * count + 6),
        out_specs=(VMEM,) * (count + 1),
        scratch_shapes=[
            pltpu.VMEM((height, NAUX), jnp.float32),
            pltpu.VMEM((height, NAUX), jnp.bfloat16),
            pltpu.VMEM((height, NAUX), jnp.bfloat16),
            pltpu.VMEM((height, width), jnp.float32),
            pltpu.VMEM((height, width), jnp.bfloat16),
            pltpu.VMEM((height, width), jnp.bfloat16),
        ],
        compiler_params=pltpu.CompilerParams(vmem_limit_bytes=56 << 20),
        name="amplitude_tile",
    )(*map(flat, f_parts), *map(flat, c_parts), *f_split, *c_split, row_pair, col_pair)
    return [v.reshape(TILES, -1, 128) for v in out[:count]], out[count]


def shards(chol, eps_occ, eps_vir):
    zh, x, c, zl, y = (lax.axis_index(a) for a in AXES)
    total = eps_vir.shape[0] * eps_occ.shape[0]

    def virtuals(places):
        ids = jnp.stack([(((h * 4 + xx % 4) * 2 + cc) * 2 + l) * 4 + yy % 4 for h, xx, cc, l, yy in places])
        return eps_vir.reshape(-1, 2)[ids].reshape(-1)

    col_places = []
    for cc in (c, 1 - c):
        here, there = (zh, zl), (1 - zh, 1 - zl)
        for (h, l), xx in (
            (here, x), (there, x), (here, x + 3), (here, x + 1),
            (here, x + 2), (there, x + 2), (there, x + 3), (there, x + 1),
        ):
            col_places.append((h, xx, cc, l, y))
    row_places = [
        (zh, x, c, l, yy)
        for l, yy in (
            (zl, y), (1 - zl, y), (zl, y + 3), (zl, y + 1),
            (zl, y + 2), (1 - zl, y + 2), (1 - zl, y + 3), (1 - zl, y + 1),
        )
    ]
    col_vir = virtuals(col_places)
    row_vir = virtuals(row_places).reshape(2, -1)
    col_pair = jnp.broadcast_to((col_vir[None, :] - eps_occ[:, None]).reshape(1, -1), (8, col_vir.shape[0] * NO))
    row_pair = (row_vir[:, None, :] - eps_occ[None, :, None]).reshape(2, -1, 1)

    half = chol.shape[0]
    chol = jnp.transpose(chol.reshape(half, TILES, 128), (1, 0, 2))
    chol_rows = chol_split = None
    factor = chol
    energies = []
    for step in range(ITERS):
        cols, rows = gather(factor, (x_step, y_step))
        cols = list(cols) + [core_swap(v) for v in cols]
        f_split = split_columns(cols)
        if step == 0:
            chol_rows, chol_split = rows, f_split
        mine, sides, far, far_sides = rows
        c_mine, c_sides, c_far, c_far_sides = chol_rows
        (p_far, p_far_sides), e_far = tile(
            (far, far_sides), (c_far, c_far_sides), f_split, chol_split, row_pair[1], col_pair, total
        )
        from_far = y_step(p_far, 2, False)
        from_sides = y_step(p_far_sides, 0, True)
        (p_mine, p_sides), e_near = tile(
            (mine, sides), (c_mine, c_sides), f_split, chol_split, row_pair[0], col_pair, total
        )
        p_mine = p_mine + from_far
        p_sides = p_sides + from_sides
        a = y_step(p_sides[:, :half], -1, False)
        b = y_step(p_sides[:, half:], 1, False)
        p = y_step(p_mine[:, half:], 0, True)
        work = p_mine[:, :half] + a + b + p
        energies.append(e_far + e_near)
        factor = chol + work

    lane = lax.broadcasted_iota(jnp.int32, (8, 128), 1)
    e = jnp.where(lane == 0, energies[0], energies[1])
    e = e + core_swap(e)
    e = e + x_step(e, 0, True)
    e = e + x_step(e, 2, False)
    e = e + x_step(e, 1, False)
    e = e + y_step(e, 0, True)
    e = e + y_step(e, 2, False)
    e = e + y_step(e, 1, False)
    work = jnp.transpose(work, (1, 0, 2)).reshape(half, -1)
    return (work, e[0, :2] / jnp.float32(total))


def solution(mesh):
    torus = Mesh(mesh.devices.reshape(2, 4, 2, 2, 4), AXES)
    placed = (P(AXES, None), P(), P())
    return jax.shard_map(
        shards, mesh=torus, in_specs=placed, out_specs=(P(AXES, None), P()), check_vma=False
    )
```

```python
import functools

import jax
import jax.numpy as jnp
from jax import lax
from jax.experimental import pallas as pl
from jax.experimental.pallas import tpu as pltpu
from jax.sharding import Mesh
from jax.sharding import PartitionSpec as P

ITERS = 2
AXES = ("zh", "x", "c", "zl", "y")
NO = 48
NAUX = 640
TILES = NAUX // 128
GROUP = 4
CHUNK = 256
VMEM = pl.BlockSpec(memory_space=pltpu.VMEM)
NT = (((1,), (1,)), ((), ()))


def x_step(v, shift, flip):
    pairs = []
    for zh in range(2):
        for x in range(4):
            for zl in range(2):
                to_zh, to_zl = (1 - zh, 1 - zl) if flip else (zh, zl)
                pairs.append(((zh * 4 + x) * 2 + zl, (to_zh * 4 + (x + shift) % 4) * 2 + to_zl))
    return lax.ppermute(v, ("zh", "x", "zl"), pairs)


def y_step(v, shift, flip):
    pairs = []
    for zl in range(2):
        for y in range(4):
            pairs.append((zl * 4 + y, (1 - zl if flip else zl) * 4 + (y + shift) % 4))
    return lax.ppermute(v, ("zl", "y"), pairs)


def core_swap(v):
    return lax.ppermute(v, "c", [(0, 1), (1, 0)])


def gather(own, steps):
    left = [s(own, 1, False) for s in steps]
    right = [s(own, -1, False) for s in steps]
    partner = [s(own, 0, True) for s in steps]
    sides = [jnp.concatenate(p, 1) for p in zip(left, right)]
    mine = [jnp.concatenate((own, p), 1) for p in partner]
    far = [s(v, 2, False) for s, v in zip(steps, mine)]
    far_sides = [s(v, 0, True) for s, v in zip(steps, sides)]
    return list(zip(mine, sides, far, far_sides))


def split(v):
    hi = v.astype(jnp.bfloat16)
    lo = (v - hi.astype(jnp.float32)).astype(jnp.bfloat16)
    return hi, lo


def occupied(k, i):
    return pl.ds(k * GROUP * NO + i, GROUP, stride=NO)


def interleave(refs, out_ref):
    count = GROUP * len(refs)

    for i in range(NO):
        for g, ref in enumerate(refs):
            at = i * count + g * GROUP
            for k in range(TILES):
                out_ref[at : at + GROUP, k * 128 : (k + 1) * 128] = ref[occupied(k, i), :]


def columns_kernel(*refs):
    parts, hi_ref, lo_ref, full = refs[:8], refs[8], refs[9], refs[10]
    interleave(parts, full)
    rows = 128

    def body(i, _):
        at = pl.ds(pl.multiple_of(i * rows, rows), rows)
        hi_ref[at, :], lo_ref[at, :] = split(full[at, :])
        return 0

    lax.fori_loop(0, full.shape[0] // rows, body, 0)


def flat(v):
    return v.reshape(-1, v.shape[2])


def split_columns(parts):
    parts = [flat(p) for p in parts]
    total = NO * GROUP * len(parts)
    shape = jax.ShapeDtypeStruct((total, NAUX), jnp.bfloat16)
    return pl.pallas_call(
        columns_kernel,
        out_shape=(shape, shape),
        in_specs=[VMEM] * len(parts),
        out_specs=(VMEM, VMEM),
        scratch_shapes=[pltpu.VMEM((total, NAUX), jnp.float32)],
        compiler_params=pltpu.CompilerParams(vmem_limit_bytes=14 << 20),
        name="split_columns",
    )(*parts)


def swap_chunks(v):
    lane = lax.broadcasted_iota(jnp.int32, v[0].shape, 1)
    low = lane < 64
    even = (lane // 32) % 2 == 0

    def halves(a, b):
        r = pltpu.roll(jnp.where(low, b, a), 64, 1)
        return jnp.where(low, a, r), jnp.where(low, r, b)

    def quarters(a, b):
        m = jnp.where(even, b, a)
        return (
            jnp.where(even, a, pltpu.roll(m, 32, 1)),
            jnp.where(even, pltpu.roll(m, 96, 1), b),
        )

    a0, a2 = halves(v[0], v[2])
    a1, a3 = halves(v[1], v[3])
    w0, w1 = quarters(a0, a1)
    w2, w3 = quarters(a2, a3)
    return w0, w1, w2, w3


def tile_kernel(count, scale, *refs):
    f_parts, c_parts = refs[:count], refs[count : 2 * count]
    (fhi, flo, chi, clo, row_pair, col_pair) = refs[2 * count : 2 * count + 6]
    outs = refs[2 * count + 6 : 3 * count + 6]
    energy = refs[3 * count + 6]
    rows, rhi, rlo, direct, *slots = refs[3 * count + 7 :]
    na = GROUP * count
    height = NO * na
    width = fhi.shape[0]
    nb = width // NO
    per = 128 // nb
    blocks = NO // per
    tall = per * na

    interleave(f_parts, rows)
    for s in range(0, height, 128):
        rhi[s : s + 128, :], rlo[s : s + 128, :] = split(rows[s : s + 128, :])

    for n in range(0, width, CHUNK):
        at = slice(n, n + CHUNK)
        acc = lax.dot_general(rhi[...], fhi[at, :], NT, preferred_element_type=jnp.float32)
        acc += lax.dot_general(rhi[...], flo[at, :], NT, preferred_element_type=jnp.float32)
        acc += lax.dot_general(rlo[...], fhi[at, :], NT, preferred_element_type=jnp.float32)
        direct[:, at] = acc

    def amplitudes(n):
        hi, lo = slots[2 * (n % 2)], slots[2 * (n % 2) + 1]
        for jj in range(CHUNK // 128):
            j = n * (CHUNK // 128) + jj
            lanes = slice(j * 128, (j + 1) * 128)
            at = slice(jj * 128, (jj + 1) * 128)
            for i in range(blocks):
                here = slice(i * tall, (i + 1) * tall)
                other = direct[j * tall : (j + 1) * tall, i * 128 : (i + 1) * 128]
                parts = [other[k * na : (k + 1) * na] for k in range(per)]
                value = direct[here, lanes]
                value = value + value - jnp.concatenate(swap_chunks(parts), 0)
                e_sum = row_pair[here, :] + col_pair[0:1, lanes]
                hi[here, at], lo[here, at] = split(value / e_sum)

    def contract(n):
        hi, lo = slots[2 * (n % 2)], slots[2 * (n % 2) + 1]
        at = slice(n * CHUNK, (n + 1) * CHUNK)
        acc = jnp.dot(hi[...], chi[at, :], preferred_element_type=jnp.float32)
        acc += jnp.dot(hi[...], clo[at, :], preferred_element_type=jnp.float32)
        acc += jnp.dot(lo[...], chi[at, :], preferred_element_type=jnp.float32)
        rows[...] = acc if n == 0 else rows[...] + acc

    chunks = width // CHUNK
    amplitudes(0)
    for n in range(chunks):
        if n + 1 < chunks:
            amplitudes(n + 1)
        contract(n)

    total = jnp.zeros((GROUP, 128), jnp.float32)
    for i in range(NO):
        for g in range(count):
            at = i * na + g * GROUP
            for k in range(TILES):
                w = rows[at : at + GROUP, k * 128 : (k + 1) * 128] * scale
                outs[g][occupied(k, i), :] = w
                total += w * c_parts[g][occupied(k, i), :]
    energy[...] = jnp.full(energy.shape, jnp.sum(total), jnp.float32)


def tile(f_parts, c_parts, f_split, c_split, row_pair, col_pair, total):
    count = len(f_parts)
    height = NO * GROUP * count
    width = f_split[0].shape[0]
    part = jax.ShapeDtypeStruct((TILES * NO * GROUP, 128), jnp.float32)
    out = pl.pallas_call(
        functools.partial(tile_kernel, count, -1.0 / total),
        out_shape=(part,) * count + (jax.ShapeDtypeStruct((8, 128), jnp.float32),),
        in_specs=[VMEM] * (2 * count + 6),
        out_specs=(VMEM,) * (count + 1),
        scratch_shapes=[
            pltpu.VMEM((height, NAUX), jnp.float32),
            pltpu.VMEM((height, NAUX), jnp.bfloat16),
            pltpu.VMEM((height, NAUX), jnp.bfloat16),
            pltpu.VMEM((height, width), jnp.float32),
        ]
        + [pltpu.VMEM((height, CHUNK), jnp.bfloat16)] * 4,
        compiler_params=pltpu.CompilerParams(vmem_limit_bytes=20 << 20),
        name="amplitude_tile",
    )(*map(flat, f_parts), *map(flat, c_parts), *f_split, *c_split, row_pair, col_pair)
    return [v.reshape(TILES, -1, 128) for v in out[:count]], out[count]


def shards(chol, eps_occ, eps_vir):
    zh, x, c, zl, y = (lax.axis_index(a) for a in AXES)
    total = eps_vir.shape[0] * eps_occ.shape[0]

    def virtuals(places):
        ids = jnp.stack([(((h * 4 + xx % 4) * 2 + cc) * 2 + l) * 4 + yy % 4 for h, xx, cc, l, yy in places])
        return eps_vir.reshape(-1, 2)[ids].reshape(-1)

    col_places = []
    for cc in (c, 1 - c):
        here, there = (zh, zl), (1 - zh, 1 - zl)
        for (h, l), xx in (
            (here, x), (there, x), (here, x + 3), (here, x + 1),
            (here, x + 2), (there, x + 2), (there, x + 3), (there, x + 1),
        ):
            col_places.append((h, xx, cc, l, y))
    row_places = [
        (zh, x, c, l, yy)
        for l, yy in (
            (zl, y), (1 - zl, y), (zl, y + 3), (zl, y + 1),
            (zl, y + 2), (1 - zl, y + 2), (1 - zl, y + 3), (1 - zl, y + 1),
        )
    ]
    col_vir = virtuals(col_places)
    row_vir = virtuals(row_places).reshape(2, -1)
    col_pair = jnp.broadcast_to((col_vir[None, :] - eps_occ[:, None]).reshape(1, -1), (8, col_vir.shape[0] * NO))
    row_pair = (row_vir[:, None, :] - eps_occ[None, :, None]).reshape(2, -1, 1)
    row_pair = jnp.broadcast_to(row_pair, row_pair.shape[:2] + (128,))

    half = chol.shape[0]
    chol = jnp.transpose(chol.reshape(half, TILES, 128), (1, 0, 2))
    chol_rows = chol_split = None
    factor = chol
    energies = []
    for step in range(ITERS):
        cols, rows = gather(factor, (x_step, y_step))
        cols = list(cols) + [core_swap(v) for v in cols]
        f_split = split_columns(cols)
        if step == 0:
            chol_rows, chol_split = rows, f_split
        mine, sides, far, far_sides = rows
        c_mine, c_sides, c_far, c_far_sides = chol_rows
        (p_far, p_far_sides), e_far = tile(
            (far, far_sides), (c_far, c_far_sides), f_split, chol_split, row_pair[1], col_pair, total
        )
        from_far = y_step(p_far, 2, False)
        from_sides = y_step(p_far_sides, 0, True)
        (p_mine, p_sides), e_near = tile(
            (mine, sides), (c_mine, c_sides), f_split, chol_split, row_pair[0], col_pair, total
        )
        p_mine = p_mine + from_far
        p_sides = p_sides + from_sides
        a = y_step(p_sides[:, :half], -1, False)
        b = y_step(p_sides[:, half:], 1, False)
        p = y_step(p_mine[:, half:], 0, True)
        work = p_mine[:, :half] + a + b + p
        energies.append(e_far + e_near)
        factor = chol + work

    lane = lax.broadcasted_iota(jnp.int32, (8, 128), 1)
    e = jnp.where(lane == 0, energies[0], energies[1])
    e = e + core_swap(e)
    e = e + x_step(e, 0, True)
    e = e + x_step(e, 1, False) + x_step(e, -1, False) + x_step(e, 2, False)
    e = e + y_step(e, 0, True)
    e = e + y_step(e, 1, False) + y_step(e, -1, False) + y_step(e, 2, False)
    work = jnp.transpose(work, (1, 0, 2)).reshape(half, -1)
    return (work, e[0, :2] / jnp.float32(total))


def solution(mesh):
    torus = Mesh(mesh.devices.reshape(2, 4, 2, 2, 4), AXES)
    placed = (P(AXES, None), P(), P())
    return jax.shard_map(
        shards, mesh=torus, in_specs=placed, out_specs=(P(AXES, None), P()), check_vma=False
    )
```

```python
import functools

import jax
import jax.numpy as jnp
from jax import lax
from jax.experimental import pallas as pl
from jax.experimental.pallas import tpu as pltpu
from jax.sharding import Mesh
from jax.sharding import PartitionSpec as P

ITERS = 2
AXES = ("zh", "x", "c", "zl", "y")
NO = 48
NAUX = 640
TILES = NAUX // 128
GROUP = 4
CHUNK = 256
LOOP_PRODUCT = (True, False)
VMEM = pl.BlockSpec(memory_space=pltpu.VMEM)
NT = (((1,), (1,)), ((), ()))


def x_step(v, shift, flip):
    pairs = []
    for zh in range(2):
        for x in range(4):
            for zl in range(2):
                to_zh, to_zl = (1 - zh, 1 - zl) if flip else (zh, zl)
                pairs.append(((zh * 4 + x) * 2 + zl, (to_zh * 4 + (x + shift) % 4) * 2 + to_zl))
    return lax.ppermute(v, ("zh", "x", "zl"), pairs)


def y_step(v, shift, flip):
    pairs = []
    for zl in range(2):
        for y in range(4):
            pairs.append((zl * 4 + y, (1 - zl if flip else zl) * 4 + (y + shift) % 4))
    return lax.ppermute(v, ("zl", "y"), pairs)


def core_swap(v):
    return lax.ppermute(v, "c", [(0, 1), (1, 0)])


def place(zh, x, c, zl, y):
    return (((zh * 4 + x % 4) * 2 + c) * 2 + zl) * 4 + y % 4


def side_step(v, shift, flip):
    pairs = []
    for zh in range(2):
        for x in range(4):
            for zl in range(2):
                for y in range(4):
                    there = 1 - zl if flip else zl
                    pairs.append((place(zh, x, 0, zl, y), place(zh, x, 0, there, y + shift)))
                    far = 1 - zh if flip else zh
                    pairs.append((place(zh, x, 1, zl, y), place(far, x + shift, 1, there, y)))
    return lax.ppermute(v, AXES, pairs)


def gather(own, core):
    pair = jnp.concatenate((own, core_swap(own)), 1)
    partner = side_step(pair, 0, True)
    left = side_step(pair, 1, False)
    right = side_step(pair, -1, False)
    near = lax.optimization_barrier([pair, partner, left, right])
    pair, partner, left, right = near
    far_left = side_step(left, 0, True)
    far_right = side_step(right, 0, True)
    far = side_step(pair, 2, False)
    far_partner = side_step(partner, 2, False)
    first = prepare(core, near, [core_swap(v) for v in near])
    far, first = lax.optimization_barrier(([far, far_partner, far_left, far_right], first))
    return [first, prepare(core, far, [core_swap(v) for v in far])]


def split(v):
    hi = v.astype(jnp.bfloat16)
    lo = (v - hi.astype(jnp.float32)).astype(jnp.bfloat16)
    return hi, lo


def occupied(i, count):
    return pl.ds(i, count, stride=NO)


def prepare_kernel(*refs):
    core, got, swapped = refs[0], refs[1:5], refs[5:9]
    col_hi, col_lo, row_hi, row_lo, rows, cols = refs[9:]
    span = GROUP * NO
    count = GROUP * len(got)
    half = GROUP // 2

    def fill(row_refs, col_refs, first):
        def tile_of(k, _):
            source = pl.ds(pl.multiple_of(k * span, 8), span)
            lanes = pl.ds(pl.multiple_of(k * 128, 128), 128)
            for i in range(NO):
                for g, ref in enumerate(col_refs):
                    at = i * count + g * GROUP
                    cols[at : at + GROUP, lanes] = ref.at[source, :][occupied(i, GROUP), :]
                for g, ref in enumerate(row_refs):
                    at = i * count // 2 + g * half
                    rows[at : at + half, lanes] = ref.at[source, :][occupied(first + i, half), :]
            return 0

        lax.fori_loop(0, TILES, tile_of, 0)

    @pl.when(core[0, 0] == 0)
    def _():
        fill(got, swapped, 0)

    @pl.when(core[0, 0] != 0)
    def _():
        fill(swapped, got, half * NO)

    def halve(source, hi, lo):
        step = 128

        def body(i, _):
            at = pl.ds(pl.multiple_of(i * step, step), step)
            hi[at, :], lo[at, :] = split(source[at, :])
            return 0

        lax.fori_loop(0, source.shape[0] // step, body, 0)

    halve(rows, row_hi, row_lo)
    halve(cols, col_hi, col_lo)


def flat(v):
    return v.reshape(-1, v.shape[2])


def prepare(core, got, swapped):
    width = NO * GROUP * len(got)
    height = width // 2
    col = jax.ShapeDtypeStruct((width, NAUX), jnp.bfloat16)
    row = jax.ShapeDtypeStruct((height, NAUX), jnp.bfloat16)
    return pl.pallas_call(
        prepare_kernel,
        out_shape=(col, col, row, row, jax.ShapeDtypeStruct(row.shape, jnp.float32)),
        in_specs=[pl.BlockSpec(memory_space=pltpu.SMEM)] + [VMEM] * (2 * len(got)),
        out_specs=(VMEM,) * 5,
        scratch_shapes=[pltpu.VMEM((width, NAUX), jnp.float32)],
        compiler_params=pltpu.CompilerParams(vmem_limit_bytes=8 << 20),
        name="prepare",
    )(core, *map(flat, got), *map(flat, swapped))


def swap_chunks(v):
    lane = lax.broadcasted_iota(jnp.int32, v[0].shape, 1)
    low = lane < 64
    even = (lane // 32) % 2 == 0

    def halves(a, b):
        r = pltpu.roll(jnp.where(low, b, a), 64, 1)
        return jnp.where(low, a, r), jnp.where(low, r, b)

    def quarters(a, b):
        m = jnp.where(even, b, a)
        return (
            jnp.where(even, a, pltpu.roll(m, 32, 1)),
            jnp.where(even, pltpu.roll(m, 96, 1), b),
        )

    a0, a2 = halves(v[0], v[2])
    a1, a3 = halves(v[1], v[3])
    w0, w1 = quarters(a0, a1)
    w2, w3 = quarters(a2, a3)
    return w0, w1, w2, w3


def tile_kernel(count, scale, *refs):
    fhi, flo, chi, clo = refs[:2], refs[2:4], refs[4:6], refs[6:8]
    rhi, rlo, c_rows, row_pair = (refs[8 + k * count : 8 + (k + 1) * count] for k in range(4))
    col_pair = refs[8 + 4 * count]
    outs = refs[9 + 4 * count : 9 + 6 * count]
    energy, rows, direct, *slots = refs[9 + 6 * count :]
    na = 8
    block = NO * na
    width = direct.shape[1]
    nb = width // NO
    per = 128 // nb
    blocks = NO // per
    tall = per * na

    def span(start, size):
        if isinstance(start, int):
            return slice(start, start + size)
        return pl.ds(pl.multiple_of(start, size), size)

    def chunk(pair, n):
        piece = nb // len(pair)
        first = n * (CHUNK // nb)
        return jnp.concatenate(
            [r[span((first + i) * piece, piece), :] for i in range(CHUNK // nb) for r in pair], 0
        )

    def product(n, _):
        hi, lo = chunk(fhi, n), chunk(flo, n)
        for g in range(count):
            acc = lax.dot_general(rhi[g][...], hi, NT, preferred_element_type=jnp.float32)
            acc += lax.dot_general(rhi[g][...], lo, NT, preferred_element_type=jnp.float32)
            acc += lax.dot_general(rlo[g][...], hi, NT, preferred_element_type=jnp.float32)
            direct[g * block : (g + 1) * block, span(n * CHUNK, CHUNK)] = acc
        return 0

    chunks = width // CHUNK
    if LOOP_PRODUCT[count - 1]:
        lax.fori_loop(0, chunks, product, 0)
    else:
        for n in range(chunks):
            product(n, 0)

    def amplitudes(n, slot):
        hi, lo = slots[2 * slot], slots[2 * slot + 1]
        for jj in range(CHUNK // 128):
            j = n * (CHUNK // 128) + jj
            lanes = span(j * 128, 128)
            at = slice(jj * 128, (jj + 1) * 128)
            for g in range(count):
                top = g * block
                for i in range(blocks):
                    here = slice(top + i * tall, top + (i + 1) * tall)
                    other = direct[span(top + j * tall, tall), i * 128 : (i + 1) * 128]
                    parts = [other[k * na : (k + 1) * na] for k in range(per)]
                    value = direct[here, lanes]
                    value = value + value - jnp.concatenate(swap_chunks(parts), 0)
                    e_sum = row_pair[g][i * tall : (i + 1) * tall, :] + col_pair[0:1, lanes]
                    hi[here, at], lo[here, at] = split(value / e_sum)

    def contract(n, slot):
        hi, lo = slots[2 * slot], slots[2 * slot + 1]
        right = chunk(chi, n)
        acc = jnp.dot(hi[...], right, preferred_element_type=jnp.float32)
        acc += jnp.dot(hi[...], chunk(clo, n), preferred_element_type=jnp.float32)
        acc += jnp.dot(lo[...], right, preferred_element_type=jnp.float32)
        rows[...] += acc

    def two_chunks(m, _):
        amplitudes(2 * m + 1, 1)
        contract(2 * m, 0)
        amplitudes(2 * m + 2, 0)
        contract(2 * m + 1, 1)
        return 0

    last = chunks - 1
    rows[...] = jnp.zeros_like(rows)
    amplitudes(0, 0)
    for m in range(last // 2):
        two_chunks(m, 0)
    amplitudes(last, 1)
    contract(last - 1, 0)
    contract(last, 1)

    def finish(k, total):
        target = pl.ds(pl.multiple_of(k * GROUP * NO, 8), GROUP * NO)
        lanes = pl.ds(pl.multiple_of(k * 128, 128), 128)
        for i in range(count * NO):
            w = rows[i * na : (i + 1) * na, lanes] * scale
            g, o = i // NO, i % NO
            for h in range(2):
                out = outs[g * 2 + h].at[target, :]
                out[occupied(o, GROUP), :] = w[h * GROUP : (h + 1) * GROUP]
            total += w * c_rows[g][o * na : (o + 1) * na, lanes]
        return total

    total = lax.fori_loop(0, TILES, finish, jnp.zeros((na, 128), jnp.float32))
    energy[...] = jnp.full(energy.shape, jnp.sum(total), jnp.float32)


def tile(groups, factor, chol, row_pair, col_pair, total):
    count = len(groups)
    height = 8 * NO * count
    width = 2 * factor[0][0].shape[0]
    part = jax.ShapeDtypeStruct((TILES * NO * GROUP, 128), jnp.float32)
    out = pl.pallas_call(
        functools.partial(tile_kernel, count, -1.0 / total),
        out_shape=(part,) * (2 * count) + (jax.ShapeDtypeStruct((8, 128), jnp.float32),),
        in_specs=[VMEM] * (9 + 4 * count),
        out_specs=(VMEM,) * (2 * count + 1),
        scratch_shapes=[
            pltpu.VMEM((height, NAUX), jnp.float32),
            pltpu.VMEM((height, width), jnp.float32),
        ]
        + [pltpu.VMEM((height, CHUNK), jnp.bfloat16)] * 4,
        compiler_params=pltpu.CompilerParams(vmem_limit_bytes=(8 if count == 1 else 14) << 20),
        name="amplitude_tile",
    )(
        *[f[0] for f in factor], *[f[1] for f in factor],
        *[c[0] for c in chol], *[c[1] for c in chol],
        *[factor[g][2] for g in groups], *[factor[g][3] for g in groups],
        *[chol[g][4] for g in groups], *[row_pair[g] for g in groups], col_pair,
    )
    return [v.reshape(TILES, -1, 128) for v in out[: 2 * count]], out[2 * count]


def shards(chol, eps_occ, eps_vir):
    zh, x, c, zl, y = (lax.axis_index(a) for a in AXES)
    total = eps_vir.shape[0] * eps_occ.shape[0]

    def virtuals(places):
        ids = jnp.stack([place(*p) for p in places])
        return eps_vir.reshape(-1, 2)[ids].reshape(-1)

    order = ((0, 0), (1, 0), (0, 3), (0, 1), (0, 2), (1, 2), (1, 3), (1, 1))
    col_vir = virtuals(
        [(zh ^ f, x + d, cc, zl ^ f, y) for f, d in order for cc in (1, 0)]
    )
    row_vir = virtuals([(zh, x, c, zl ^ f, y + d) for f, d in order]).reshape(2, -1)
    col_pair = jnp.broadcast_to((col_vir[None, :] - eps_occ[:, None]).reshape(1, -1), (8, col_vir.shape[0] * NO))
    row_pair = (row_vir[:, None, :] - eps_occ[None, :, None]).reshape(2, -1, 1)
    row_pair = jnp.broadcast_to(row_pair, row_pair.shape[:2] + (128,))

    half = chol.shape[0]
    chol = jnp.transpose(chol.reshape(half, TILES, 128), (1, 0, 2))
    core = c.astype(jnp.int32).reshape(1, 1)
    chol_parts = None
    factor = chol
    energies = []
    for step in range(ITERS):
        factor_parts = gather(factor, core)
        if step == 0:
            chol_parts = factor_parts
        if step < ITERS - 1:
            (p_far, p_far_sides), e_far = tile((1,), factor_parts, chol_parts, row_pair, col_pair, total)
            (p_mine, p_sides), e_near = tile((0,), factor_parts, chol_parts, row_pair, col_pair, total)
            energies.append(e_far + e_near)
        else:
            (p_mine, p_sides, p_far, p_far_sides), e_all = tile(
                (0, 1), factor_parts, chol_parts, row_pair, col_pair, total
            )
            energies.append(e_all)
        p_mine = p_mine + y_step(p_far, 2, False)
        p_sides = p_sides + y_step(p_far_sides, 0, True)
        to_left, to_right, to_partner = p_sides[:, :half], p_sides[:, half:], p_mine[:, half:]
        if step == ITERS - 1:
            lane = lax.broadcasted_iota(jnp.int32, (8, 128), 1)
            e = jnp.where(lane == 0, energies[0], energies[1])
            e = e + core_swap(e)
            e = e + x_step(e, 0, True)
            e = e + y_step(e, 2, True)
            tail = jnp.broadcast_to(e[None], (TILES, 8, 128))
            to_left, to_right, to_partner = (
                jnp.concatenate((v, tail), 1) for v in (to_left, to_right, to_partner)
            )
        a = y_step(to_left, -1, False)
        b = y_step(to_right, 1, False)
        p = y_step(to_partner, 0, True)
        work = p_mine[:, :half] + a[:, :half] + b[:, :half] + p[:, :half]
        factor = chol + work

    e = e + a[0, half:] + b[0, half:] + p[0, half:]
    e = e + x_step(e, 1, False) + x_step(e, -1, False) + x_step(e, 2, False)
    work = jnp.transpose(work, (1, 0, 2)).reshape(half, -1)
    return (work, e[0, :2] / jnp.float32(total))


def solution(mesh):
    torus = Mesh(mesh.devices.reshape(2, 4, 2, 2, 4), AXES)
    placed = (P(AXES, None), P(), P())
    return jax.shard_map(
        shards, mesh=torus, in_specs=placed, out_specs=(P(AXES, None), P()), check_vma=False
    )
```

```python
import functools

import jax
import jax.numpy as jnp
from jax import lax
from jax.experimental import pallas as pl
from jax.experimental.pallas import tpu as pltpu
from jax.sharding import Mesh
from jax.sharding import PartitionSpec as P

ITERS = 2
AXES = ("zh", "x", "c", "zl", "y")
NO = 48
NAUX = 640
TILES = NAUX // 128
GROUP = 4
CHUNK = 256
LOOP_PRODUCT = (True, False)
VMEM = pl.BlockSpec(memory_space=pltpu.VMEM)
NT = (((1,), (1,)), ((), ()))


def y_step(v, shift, flip):
    pairs = []
    for zl in range(2):
        for y in range(4):
            pairs.append((zl * 4 + y, (1 - zl if flip else zl) * 4 + (y + shift) % 4))
    return lax.ppermute(v, ("zl", "y"), pairs)


def core_swap(v):
    return lax.ppermute(v, "c", [(0, 1), (1, 0)])


def place(zh, x, c, zl, y):
    return (((zh * 4 + x % 4) * 2 + c) * 2 + zl) * 4 + y % 4


def hop(v, flip_zh, shift_x, flip_zl, shift_y):
    pairs = [
        (place(zh, x, c, zl, y), place(zh ^ flip_zh, x + shift_x, c, zl ^ flip_zl, y + shift_y))
        for zh in range(2) for x in range(4) for c in range(2) for zl in range(2) for y in range(4)
    ]
    return lax.ppermute(v, AXES, pairs)


def side_step(v, shift, flip):
    pairs = []
    for zh in range(2):
        for x in range(4):
            for zl in range(2):
                for y in range(4):
                    there = 1 - zl if flip else zl
                    pairs.append((place(zh, x, 0, zl, y), place(zh, x, 0, there, y + shift)))
                    far = 1 - zh if flip else zh
                    pairs.append((place(zh, x, 1, zl, y), place(far, x + shift, 1, there, y)))
    return lax.ppermute(v, AXES, pairs)


def gather(own, core):
    pair = jnp.concatenate((own, core_swap(own)), 1)
    partner = side_step(pair, 0, True)
    left = side_step(pair, 1, False)
    right = side_step(pair, -1, False)
    near = [pair, partner, left, right]
    far_left = side_step(left, 0, True)
    far_right = side_step(right, 0, True)
    far = side_step(lax.optimization_barrier((pair, left, right))[0], 2, False)
    far_partner = side_step(partner, 2, False)
    first = prepare(core, near, [core_swap(v) for v in near])
    far = [far, far_partner, far_left, far_right]
    far = [lax.optimization_barrier((v, first))[0] for v in far]
    return [first, prepare(core, far, [core_swap(v) for v in far])]


def split(v):
    hi = v.astype(jnp.bfloat16)
    lo = (v - hi.astype(jnp.float32)).astype(jnp.bfloat16)
    return hi, lo


def occupied(i, count):
    return pl.ds(i, count, stride=NO)


def prepare_kernel(*refs):
    core, got, swapped = refs[0], refs[1:5], refs[5:9]
    col_hi, col_lo, row_hi, row_lo, rows, cols = refs[9:]
    span = GROUP * NO
    count = GROUP * len(got)
    half = GROUP // 2

    def fill(row_refs, col_refs, first):
        def tile_of(k, _):
            source = pl.ds(pl.multiple_of(k * span, 8), span)
            lanes = pl.ds(pl.multiple_of(k * 128, 128), 128)
            for i in range(NO):
                for g, ref in enumerate(col_refs):
                    at = i * count + g * GROUP
                    cols[at : at + GROUP, lanes] = ref.at[source, :][occupied(i, GROUP), :]
                for g, ref in enumerate(row_refs):
                    at = i * count // 2 + g * half
                    rows[at : at + half, lanes] = ref.at[source, :][occupied(first + i, half), :]
            return 0

        lax.fori_loop(0, TILES, tile_of, 0)

    @pl.when(core[0, 0] == 0)
    def _():
        fill(got, swapped, 0)

    @pl.when(core[0, 0] != 0)
    def _():
        fill(swapped, got, half * NO)

    def halve(source, hi, lo):
        step = 128

        def body(i, _):
            at = pl.ds(pl.multiple_of(i * step, step), step)
            hi[at, :], lo[at, :] = split(source[at, :])
            return 0

        lax.fori_loop(0, source.shape[0] // step, body, 0)

    halve(rows, row_hi, row_lo)
    halve(cols, col_hi, col_lo)


def flat(v):
    return v.reshape(-1, v.shape[2])


def prepare(core, got, swapped):
    width = NO * GROUP * len(got)
    height = width // 2
    col = jax.ShapeDtypeStruct((width, NAUX), jnp.bfloat16)
    row = jax.ShapeDtypeStruct((height, NAUX), jnp.bfloat16)
    return pl.pallas_call(
        prepare_kernel,
        out_shape=(col, col, row, row, jax.ShapeDtypeStruct(row.shape, jnp.float32)),
        in_specs=[pl.BlockSpec(memory_space=pltpu.SMEM)] + [VMEM] * (2 * len(got)),
        out_specs=(VMEM,) * 5,
        scratch_shapes=[pltpu.VMEM((width, NAUX), jnp.float32)],
        compiler_params=pltpu.CompilerParams(vmem_limit_bytes=8 << 20),
        name="prepare",
    )(core, *map(flat, got), *map(flat, swapped))


def swap_chunks(v):
    lane = lax.broadcasted_iota(jnp.int32, v[0].shape, 1)
    low = lane < 64
    even = (lane // 32) % 2 == 0

    def halves(a, b):
        r = pltpu.roll(jnp.where(low, b, a), 64, 1)
        return jnp.where(low, a, r), jnp.where(low, r, b)

    def quarters(a, b):
        m = jnp.where(even, b, a)
        return (
            jnp.where(even, a, pltpu.roll(m, 32, 1)),
            jnp.where(even, pltpu.roll(m, 96, 1), b),
        )

    a0, a2 = halves(v[0], v[2])
    a1, a3 = halves(v[1], v[3])
    w0, w1 = quarters(a0, a1)
    w2, w3 = quarters(a2, a3)
    return w0, w1, w2, w3


def tile_kernel(count, scale, *refs):
    fhi, flo, chi, clo = refs[:2], refs[2:4], refs[4:6], refs[6:8]
    rhi, rlo, c_rows, row_pair = (refs[8 + k * count : 8 + (k + 1) * count] for k in range(4))
    col_pair = refs[8 + 4 * count]
    outs = refs[9 + 4 * count : 9 + 6 * count]
    energy, rows, direct, *slots = refs[9 + 6 * count :]
    na = 8
    block = NO * na
    width = direct.shape[1]
    nb = width // NO
    per = 128 // nb
    blocks = NO // per
    tall = per * na

    def span(start, size):
        if isinstance(start, int):
            return slice(start, start + size)
        return pl.ds(pl.multiple_of(start, size), size)

    def chunk(pair, n):
        piece = nb // len(pair)
        first = n * (CHUNK // nb)
        return jnp.concatenate(
            [r[span((first + i) * piece, piece), :] for i in range(CHUNK // nb) for r in pair], 0
        )

    def product(n, _):
        hi, lo = chunk(fhi, n), chunk(flo, n)
        for g in range(count):
            acc = lax.dot_general(rhi[g][...], hi, NT, preferred_element_type=jnp.float32)
            acc += lax.dot_general(rhi[g][...], lo, NT, preferred_element_type=jnp.float32)
            acc += lax.dot_general(rlo[g][...], hi, NT, preferred_element_type=jnp.float32)
            direct[g * block : (g + 1) * block, span(n * CHUNK, CHUNK)] = acc
        return 0

    chunks = width // CHUNK
    if LOOP_PRODUCT[count - 1]:
        lax.fori_loop(0, chunks, product, 0)
    else:
        for n in range(chunks):
            product(n, 0)

    def amplitudes(n, slot):
        hi, lo = slots[2 * slot], slots[2 * slot + 1]
        for jj in range(CHUNK // 128):
            j = n * (CHUNK // 128) + jj
            lanes = span(j * 128, 128)
            at = slice(jj * 128, (jj + 1) * 128)
            for g in range(count):
                top = g * block
                for i in range(blocks):
                    here = slice(top + i * tall, top + (i + 1) * tall)
                    other = direct[span(top + j * tall, tall), i * 128 : (i + 1) * 128]
                    parts = [other[k * na : (k + 1) * na] for k in range(per)]
                    value = direct[here, lanes]
                    value = value + value - jnp.concatenate(swap_chunks(parts), 0)
                    e_sum = row_pair[g][i * tall : (i + 1) * tall, :] + col_pair[0:1, lanes]
                    hi[here, at], lo[here, at] = split(value / e_sum)

    def contract(n, slot):
        hi, lo = slots[2 * slot], slots[2 * slot + 1]
        right = chunk(chi, n)
        acc = jnp.dot(hi[...], right, preferred_element_type=jnp.float32)
        acc += jnp.dot(hi[...], chunk(clo, n), preferred_element_type=jnp.float32)
        acc += jnp.dot(lo[...], right, preferred_element_type=jnp.float32)
        rows[...] += acc

    def two_chunks(m, _):
        amplitudes(2 * m + 1, 1)
        contract(2 * m, 0)
        amplitudes(2 * m + 2, 0)
        contract(2 * m + 1, 1)
        return 0

    last = chunks - 1
    rows[...] = jnp.zeros_like(rows)
    amplitudes(0, 0)
    for m in range(last // 2):
        two_chunks(m, 0)
    amplitudes(last, 1)
    contract(last - 1, 0)
    contract(last, 1)

    def finish(k, total):
        target = pl.ds(pl.multiple_of(k * GROUP * NO, 8), GROUP * NO)
        lanes = pl.ds(pl.multiple_of(k * 128, 128), 128)
        for i in range(count * NO):
            w = rows[i * na : (i + 1) * na, lanes] * scale
            g, o = i // NO, i % NO
            for h in range(2):
                out = outs[g * 2 + h].at[target, :]
                out[occupied(o, GROUP), :] = w[h * GROUP : (h + 1) * GROUP]
            total += w * c_rows[g][o * na : (o + 1) * na, lanes]
        return total

    total = lax.fori_loop(0, TILES, finish, jnp.zeros((na, 128), jnp.float32))
    energy[...] = jnp.full(energy.shape, jnp.sum(total), jnp.float32)


def tile(groups, factor, chol, row_pair, col_pair, total):
    count = len(groups)
    height = 8 * NO * count
    width = 2 * factor[0][0].shape[0]
    part = jax.ShapeDtypeStruct((TILES * NO * GROUP, 128), jnp.float32)
    out = pl.pallas_call(
        functools.partial(tile_kernel, count, -1.0 / total),
        out_shape=(part,) * (2 * count) + (jax.ShapeDtypeStruct((8, 128), jnp.float32),),
        in_specs=[VMEM] * (9 + 4 * count),
        out_specs=(VMEM,) * (2 * count + 1),
        scratch_shapes=[
            pltpu.VMEM((height, NAUX), jnp.float32),
            pltpu.VMEM((height, width), jnp.float32),
        ]
        + [pltpu.VMEM((height, CHUNK), jnp.bfloat16)] * 4,
        compiler_params=pltpu.CompilerParams(vmem_limit_bytes=(8 if count == 1 else 14) << 20),
        name="amplitude_tile",
    )(
        *[f[0] for f in factor], *[f[1] for f in factor],
        *[c[0] for c in chol], *[c[1] for c in chol],
        *[factor[g][2] for g in groups], *[factor[g][3] for g in groups],
        *[chol[g][4] for g in groups], *[row_pair[g] for g in groups], col_pair,
    )
    return [v.reshape(TILES, -1, 128) for v in out[: 2 * count]], out[2 * count]


def shards(chol, eps_occ, eps_vir):
    zh, x, c, zl, y = (lax.axis_index(a) for a in AXES)
    total = eps_vir.shape[0] * eps_occ.shape[0]

    def virtuals(places):
        ids = jnp.stack([place(*p) for p in places])
        return eps_vir.reshape(-1, 2)[ids].reshape(-1)

    order = ((0, 0), (1, 0), (0, 3), (0, 1), (0, 2), (1, 2), (1, 3), (1, 1))
    col_vir = virtuals(
        [(zh ^ f, x + d, cc, zl ^ f, y) for f, d in order for cc in (1, 0)]
    )
    row_vir = virtuals([(zh, x, c, zl ^ f, y + d) for f, d in order]).reshape(2, -1)
    col_pair = jnp.broadcast_to((col_vir[None, :] - eps_occ[:, None]).reshape(1, -1), (8, col_vir.shape[0] * NO))
    row_pair = (row_vir[:, None, :] - eps_occ[None, :, None]).reshape(2, -1, 1)
    row_pair = jnp.broadcast_to(row_pair, row_pair.shape[:2] + (128,))

    half = chol.shape[0]
    chol = jnp.transpose(chol.reshape(half, TILES, 128), (1, 0, 2))
    core = c.astype(jnp.int32).reshape(1, 1)
    chol_parts = None
    factor = chol
    energies = []
    for step in range(ITERS):
        factor_parts = gather(factor, core)
        if step == 0:
            chol_parts = factor_parts
        if step < ITERS - 1:
            (p_far, p_far_sides), e_far = tile((1,), factor_parts, chol_parts, row_pair, col_pair, total)
            (p_mine, p_sides), e_near = tile((0,), factor_parts, chol_parts, row_pair, col_pair, total)
            energies.append(e_far + e_near)
        else:
            (p_mine, p_sides, p_far, p_far_sides), e_all = tile(
                (0, 1), factor_parts, chol_parts, row_pair, col_pair, total
            )
            energies.append(e_all)
        p_mine = p_mine + y_step(p_far, 2, False)
        p_sides = p_sides + y_step(p_far_sides, 0, True)
        to_left, to_right, to_partner = p_sides[:, :half], p_sides[:, half:], p_mine[:, half:]
        if step == ITERS - 1:
            lane = lax.broadcasted_iota(jnp.int32, (8, 128), 1)
            e = jnp.where(lane == 0, energies[0], energies[1])
            e = e + core_swap(e)
            e = e + hop(e, 1, 0, 1, 0) + hop(e, 0, 0, 1, 2) + hop(e, 1, 0, 0, 2)
            e = e + hop(e, 0, 1, 0, 0) + hop(e, 0, 3, 0, 0) + hop(e, 0, 2, 0, 0)
            tail = jnp.broadcast_to(e[None], (TILES, 8, 128))
            to_left, to_right, to_partner = (
                jnp.concatenate((v, tail), 1) for v in (to_left, to_right, to_partner)
            )
        a = y_step(to_left, -1, False)
        b = y_step(to_right, 1, False)
        p = y_step(to_partner, 0, True)
        work = p_mine[:, :half] + a[:, :half] + b[:, :half] + p[:, :half]
        factor = chol + work

    e = e + a[0, half:] + b[0, half:] + p[0, half:]
    work = jnp.transpose(work, (1, 0, 2)).reshape(half, -1)
    return (work, e[0, :2] / jnp.float32(total))


def solution(mesh):
    torus = Mesh(mesh.devices.reshape(2, 4, 2, 2, 4), AXES)
    placed = (P(AXES, None), P(), P())
    return jax.shard_map(
        shards, mesh=torus, in_specs=placed, out_specs=(P(AXES, None), P()), check_vma=False
    )
```

```python
import functools

import jax
import jax.numpy as jnp
from jax import lax
from jax.experimental import pallas as pl
from jax.experimental.pallas import tpu as pltpu
from jax.sharding import Mesh
from jax.sharding import PartitionSpec as P

ITERS = 2
AXES = ("zh", "x", "c", "zl", "y")
NO = 48
NAUX = 640
TILES = NAUX // 128
GROUP = 4
CHUNK = 256
LOOP_PRODUCT = (True, False)
VMEM = pl.BlockSpec(memory_space=pltpu.VMEM)
NT = (((1,), (1,)), ((), ()))


def y_step(v, shift, flip):
    pairs = []
    for zl in range(2):
        for y in range(4):
            pairs.append((zl * 4 + y, (1 - zl if flip else zl) * 4 + (y + shift) % 4))
    return lax.ppermute(v, ("zl", "y"), pairs)


def core_swap(v):
    return lax.ppermute(v, "c", [(0, 1), (1, 0)])


def place(zh, x, c, zl, y):
    return (((zh * 4 + x % 4) * 2 + c) * 2 + zl) * 4 + y % 4


def hop(v, flip_zh, shift_x, flip_zl, shift_y):
    pairs = [
        (place(zh, x, c, zl, y), place(zh ^ flip_zh, x + shift_x, c, zl ^ flip_zl, y + shift_y))
        for zh in range(2) for x in range(4) for c in range(2) for zl in range(2) for y in range(4)
    ]
    return lax.ppermute(v, AXES, pairs)


def side_step(v, shift, flip):
    pairs = []
    for zh in range(2):
        for x in range(4):
            for zl in range(2):
                for y in range(4):
                    there = 1 - zl if flip else zl
                    pairs.append((place(zh, x, 0, zl, y), place(zh, x, 0, there, y + shift)))
                    far = 1 - zh if flip else zh
                    pairs.append((place(zh, x, 1, zl, y), place(far, x + shift, 1, there, y)))
    return lax.ppermute(v, AXES, pairs)


def gather(own, core):
    pair = jnp.concatenate((own, core_swap(own)), 1)
    partner = side_step(pair, 0, True)
    left = side_step(pair, 1, False)
    right = side_step(pair, -1, False)
    near = [pair, partner, left, right]
    far_left = side_step(left, 0, True)
    far_right = side_step(right, 0, True)
    far = side_step(lax.optimization_barrier((pair, left, right))[0], 2, False)
    far_partner = side_step(partner, 2, False)
    first = prepare(core, near, [core_swap(v) for v in near])
    far = [far, far_partner, far_left, far_right]
    far = [lax.optimization_barrier((v, first))[0] for v in far]
    return [first, prepare(core, far, [core_swap(v) for v in far])]


def split(v):
    hi = v.astype(jnp.bfloat16)
    lo = (v - hi.astype(jnp.float32)).astype(jnp.bfloat16)
    return hi, lo


def occupied(i, count):
    return pl.ds(i, count, stride=NO)


def prepare_kernel(*refs):
    core, got, swapped = refs[0], refs[1:5], refs[5:9]
    col_hi, col_lo, row_hi, row_lo, rows, cols = refs[9:]
    span = GROUP * NO
    count = GROUP * len(got)
    half = GROUP // 2

    def fill(row_refs, col_refs, first):
        def tile_of(k, _):
            source = pl.ds(pl.multiple_of(k * span, 8), span)
            lanes = pl.ds(pl.multiple_of(k * 128, 128), 128)
            for i in range(NO):
                for g, ref in enumerate(col_refs):
                    at = i * count + g * GROUP
                    cols[at : at + GROUP, lanes] = ref.at[source, :][occupied(i, GROUP), :]
                for g, ref in enumerate(row_refs):
                    at = i * count // 2 + g * half
                    rows[at : at + half, lanes] = ref.at[source, :][occupied(first + i, half), :]
            return 0

        lax.fori_loop(0, TILES, tile_of, 0)

    @pl.when(core[0, 0] == 0)
    def _():
        fill(got, swapped, 0)

    @pl.when(core[0, 0] != 0)
    def _():
        fill(swapped, got, half * NO)

    def halve(source, hi, lo):
        step = 128

        def body(i, _):
            at = pl.ds(pl.multiple_of(i * step, step), step)
            hi[at, :], lo[at, :] = split(source[at, :])
            return 0

        lax.fori_loop(0, source.shape[0] // step, body, 0)

    halve(rows, row_hi, row_lo)
    halve(cols, col_hi, col_lo)


def flat(v):
    return v.reshape(-1, v.shape[2])


def prepare(core, got, swapped):
    width = NO * GROUP * len(got)
    height = width // 2
    col = jax.ShapeDtypeStruct((width, NAUX), jnp.bfloat16)
    row = jax.ShapeDtypeStruct((height, NAUX), jnp.bfloat16)
    return pl.pallas_call(
        prepare_kernel,
        out_shape=(col, col, row, row, jax.ShapeDtypeStruct(row.shape, jnp.float32)),
        in_specs=[pl.BlockSpec(memory_space=pltpu.SMEM)] + [VMEM] * (2 * len(got)),
        out_specs=(VMEM,) * 5,
        scratch_shapes=[pltpu.VMEM((width, NAUX), jnp.float32)],
        compiler_params=pltpu.CompilerParams(vmem_limit_bytes=8 << 20),
        name="prepare",
    )(core, *map(flat, got), *map(flat, swapped))


def swap_chunks(v):
    lane = lax.broadcasted_iota(jnp.int32, v[0].shape, 1)
    low = lane < 64
    even = (lane // 32) % 2 == 0

    def halves(a, b):
        r = pltpu.roll(jnp.where(low, b, a), 64, 1)
        return jnp.where(low, a, r), jnp.where(low, r, b)

    def quarters(a, b):
        m = jnp.where(even, b, a)
        return (
            jnp.where(even, a, pltpu.roll(m, 32, 1)),
            jnp.where(even, pltpu.roll(m, 96, 1), b),
        )

    a0, a2 = halves(v[0], v[2])
    a1, a3 = halves(v[1], v[3])
    w0, w1 = quarters(a0, a1)
    w2, w3 = quarters(a2, a3)
    return w0, w1, w2, w3


def tile_kernel(count, scale, *refs):
    fhi, flo, chi, clo = refs[:2], refs[2:4], refs[4:6], refs[6:8]
    rhi, rlo, c_rows, row_pair = (refs[8 + k * count : 8 + (k + 1) * count] for k in range(4))
    col_pair = refs[8 + 4 * count]
    outs = refs[9 + 4 * count : 9 + 6 * count]
    energy, rows, direct, *slots = refs[9 + 6 * count :]
    na = 8
    block = NO * na
    width = direct.shape[1]
    nb = width // NO
    per = 128 // nb
    blocks = NO // per
    tall = per * na

    def span(start, size):
        if isinstance(start, int):
            return slice(start, start + size)
        return pl.ds(pl.multiple_of(start, size), size)

    def chunk(pair, n):
        piece = nb // len(pair)
        first = n * (CHUNK // nb)
        return jnp.concatenate(
            [r[span((first + i) * piece, piece), :] for i in range(CHUNK // nb) for r in pair], 0
        )

    def product(n, _):
        hi, lo = chunk(fhi, n), chunk(flo, n)
        for g in range(count):
            acc = lax.dot_general(rhi[g][...], hi, NT, preferred_element_type=jnp.float32)
            acc += lax.dot_general(rhi[g][...], lo, NT, preferred_element_type=jnp.float32)
            acc += lax.dot_general(rlo[g][...], hi, NT, preferred_element_type=jnp.float32)
            direct[g * block : (g + 1) * block, span(n * CHUNK, CHUNK)] = acc
        return 0

    chunks = width // CHUNK
    if LOOP_PRODUCT[count - 1]:
        lax.fori_loop(0, chunks, product, 0)
    else:
        for n in range(chunks):
            product(n, 0)

    def amplitudes(n, slot):
        hi, lo = slots[2 * slot], slots[2 * slot + 1]
        for jj in range(CHUNK // 128):
            j = n * (CHUNK // 128) + jj
            lanes = span(j * 128, 128)
            at = slice(jj * 128, (jj + 1) * 128)
            for g in range(count):
                top = g * block
                for i in range(blocks):
                    here = slice(top + i * tall, top + (i + 1) * tall)
                    other = direct[span(top + j * tall, tall), i * 128 : (i + 1) * 128]
                    parts = [other[k * na : (k + 1) * na] for k in range(per)]
                    value = direct[here, lanes]
                    value = value + value - jnp.concatenate(swap_chunks(parts), 0)
                    e_sum = row_pair[g][i * tall : (i + 1) * tall, :] + col_pair[0:1, lanes]
                    hi[here, at], lo[here, at] = split(value / e_sum)

    def contract(n, slot):
        hi, lo = slots[2 * slot], slots[2 * slot + 1]
        right = chunk(chi, n)
        acc = jnp.dot(hi[...], right, preferred_element_type=jnp.float32)
        acc += jnp.dot(hi[...], chunk(clo, n), preferred_element_type=jnp.float32)
        acc += jnp.dot(lo[...], right, preferred_element_type=jnp.float32)
        rows[...] += acc

    def two_chunks(m, _):
        amplitudes(2 * m + 1, 1)
        contract(2 * m, 0)
        amplitudes(2 * m + 2, 0)
        contract(2 * m + 1, 1)
        return 0

    last = chunks - 1
    rows[...] = jnp.zeros_like(rows)
    amplitudes(0, 0)
    for m in range(last // 2):
        two_chunks(m, 0)
    amplitudes(last, 1)
    contract(last - 1, 0)
    contract(last, 1)

    def finish(k, total):
        target = pl.ds(pl.multiple_of(k * GROUP * NO, 8), GROUP * NO)
        lanes = pl.ds(pl.multiple_of(k * 128, 128), 128)
        for i in range(count * NO):
            w = rows[i * na : (i + 1) * na, lanes] * scale
            g, o = i // NO, i % NO
            for h in range(2):
                out = outs[g * 2 + h].at[target, :]
                out[occupied(o, GROUP), :] = w[h * GROUP : (h + 1) * GROUP]
            total += w * c_rows[g][o * na : (o + 1) * na, lanes]
        return total

    total = lax.fori_loop(0, TILES, finish, jnp.zeros((na, 128), jnp.float32))
    energy[...] = jnp.full(energy.shape, jnp.sum(total), jnp.float32)


def tile(groups, factor, chol, row_pair, col_pair, total):
    count = len(groups)
    height = 8 * NO * count
    width = 2 * factor[0][0].shape[0]
    part = jax.ShapeDtypeStruct((TILES * NO * GROUP, 128), jnp.float32)
    out = pl.pallas_call(
        functools.partial(tile_kernel, count, -1.0 / total),
        out_shape=(part,) * (2 * count) + (jax.ShapeDtypeStruct((8, 128), jnp.float32),),
        in_specs=[VMEM] * (9 + 4 * count),
        out_specs=(VMEM,) * (2 * count + 1),
        scratch_shapes=[
            pltpu.VMEM((height, NAUX), jnp.float32),
            pltpu.VMEM((height, width), jnp.float32),
        ]
        + [pltpu.VMEM((height, CHUNK), jnp.bfloat16)] * 4,
        compiler_params=pltpu.CompilerParams(vmem_limit_bytes=(8 if count == 1 else 14) << 20),
        name="amplitude_tile",
    )(
        *[f[0] for f in factor], *[f[1] for f in factor],
        *[c[0] for c in chol], *[c[1] for c in chol],
        *[factor[g][2] for g in groups], *[factor[g][3] for g in groups],
        *[chol[g][4] for g in groups], *[row_pair[g] for g in groups], col_pair,
    )
    return [v.reshape(TILES, -1, 128) for v in out[: 2 * count]], out[2 * count]


def shards(chol, eps_occ, eps_vir):
    zh, x, c, zl, y = (lax.axis_index(a) for a in AXES)
    total = eps_vir.shape[0] * eps_occ.shape[0]

    def virtuals(places):
        ids = jnp.stack([place(*p) for p in places])
        return eps_vir.reshape(-1, 2)[ids].reshape(-1)

    order = ((0, 0), (1, 0), (0, 3), (0, 1), (0, 2), (1, 2), (1, 3), (1, 1))
    col_vir = virtuals(
        [(zh ^ f, x + d, cc, zl ^ f, y) for f, d in order for cc in (1, 0)]
    )
    row_vir = virtuals([(zh, x, c, zl ^ f, y + d) for f, d in order]).reshape(2, -1)
    col_pair = jnp.broadcast_to((col_vir[None, :] - eps_occ[:, None]).reshape(1, -1), (8, col_vir.shape[0] * NO))
    row_pair = (row_vir[:, None, :] - eps_occ[None, :, None]).reshape(2, -1, 1)
    row_pair = jnp.broadcast_to(row_pair, row_pair.shape[:2] + (128,))

    half = chol.shape[0]
    chol = jnp.transpose(chol.reshape(half, TILES, 128), (1, 0, 2))
    core = c.astype(jnp.int32).reshape(1, 1)
    chol_parts = None
    factor = chol
    energies = []
    for step in range(ITERS):
        factor_parts = gather(factor, core)
        if step == 0:
            chol_parts = factor_parts
        if step < ITERS - 1:
            (p_far, p_far_sides), e_far = tile((1,), factor_parts, chol_parts, row_pair, col_pair, total)
            (p_mine, p_sides), e_near = tile((0,), factor_parts, chol_parts, row_pair, col_pair, total)
            energies.append(e_far + e_near)
        else:
            (p_mine, p_sides, p_far, p_far_sides), e_all = tile(
                (0, 1), factor_parts, chol_parts, row_pair, col_pair, total
            )
            energies.append(e_all)
        p_mine = p_mine + y_step(p_far, 2, False)
        p_sides = p_sides + y_step(p_far_sides, 0, True)
        to_left, to_right, to_partner = p_sides[:, :half], p_sides[:, half:], p_mine[:, half:]
        if step == ITERS - 1:
            lane = lax.broadcasted_iota(jnp.int32, (8, 128), 1)
            e = jnp.where(lane == 0, energies[0], energies[1])
            e = e + core_swap(e)
            e = e + hop(e, 0, 1, 0, 0) + hop(e, 0, 3, 0, 0) + hop(e, 0, 2, 0, 0)
            e = e + hop(e, 1, 0, 1, 0) + hop(e, 0, 0, 1, 2) + hop(e, 1, 0, 0, 2)
            tail = jnp.broadcast_to(e[None], (TILES, 8, 128))
            to_left, to_right, to_partner = (
                jnp.concatenate((v, tail), 1) for v in (to_left, to_right, to_partner)
            )
        a = y_step(to_left, -1, False)
        b = y_step(to_right, 1, False)
        p = y_step(to_partner, 0, True)
        work = p_mine[:, :half] + a[:, :half] + b[:, :half] + p[:, :half]
        factor = chol + work

    e = e + a[0, half:] + b[0, half:] + p[0, half:]
    work = jnp.transpose(work, (1, 0, 2)).reshape(half, -1)
    return (work, e[0, :2] / jnp.float32(total))


def solution(mesh):
    torus = Mesh(mesh.devices.reshape(2, 4, 2, 2, 4), AXES)
    placed = (P(AXES, None), P(), P())
    return jax.shard_map(
        shards, mesh=torus, in_specs=placed, out_specs=(P(AXES, None), P()), check_vma=False
    )
```

```python
import functools

import jax
import jax.numpy as jnp
from jax import lax
from jax.experimental import pallas as pl
from jax.experimental.pallas import tpu as pltpu
from jax.sharding import Mesh
from jax.sharding import PartitionSpec as P

ITERS = 2
AXES = ("zh", "x", "c", "zl", "y")
NO = 48
NAUX = 640
TILES = NAUX // 128
GROUP = 4
CHUNK = 256
LOOP_PRODUCT = (True, False)
VMEM = pl.BlockSpec(memory_space=pltpu.VMEM)
NT = (((1,), (1,)), ((), ()))


def y_step(v, shift, flip):
    pairs = []
    for zl in range(2):
        for y in range(4):
            pairs.append((zl * 4 + y, (1 - zl if flip else zl) * 4 + (y + shift) % 4))
    return lax.ppermute(v, ("zl", "y"), pairs)


def core_swap(v):
    return lax.ppermute(v, "c", [(0, 1), (1, 0)])


def place(zh, x, c, zl, y):
    return (((zh * 4 + x % 4) * 2 + c) * 2 + zl) * 4 + y % 4


def hop(v, flip_zh, shift_x, flip_zl, shift_y):
    pairs = [
        (place(zh, x, c, zl, y), place(zh ^ flip_zh, x + shift_x, c, zl ^ flip_zl, y + shift_y))
        for zh in range(2) for x in range(4) for c in range(2) for zl in range(2) for y in range(4)
    ]
    return lax.ppermute(v, AXES, pairs)


def side_step(v, shift, flip):
    pairs = []
    for zh in range(2):
        for x in range(4):
            for zl in range(2):
                for y in range(4):
                    there = 1 - zl if flip else zl
                    pairs.append((place(zh, x, 0, zl, y), place(zh, x, 0, there, y + shift)))
                    far = 1 - zh if flip else zh
                    pairs.append((place(zh, x, 1, zl, y), place(far, x + shift, 1, there, y)))
    return lax.ppermute(v, AXES, pairs)


def gather(own, core):
    pair = jnp.concatenate((own, core_swap(own)), 1)
    partner = side_step(pair, 0, True)
    left = side_step(pair, 1, False)
    right = side_step(pair, -1, False)
    near = [pair, partner, left, right]
    far_left = side_step(left, 0, True)
    far_right = side_step(right, 0, True)
    far = side_step(lax.optimization_barrier((pair, left, right))[0], 2, False)
    far_partner = side_step(partner, 2, False)
    first = prepare(core, near, [core_swap(v) for v in near])
    far = [far, far_partner, far_left, far_right]
    far = [lax.optimization_barrier((v, first))[0] for v in far]
    return [first, prepare(core, far, [core_swap(v) for v in far])]


def split(v):
    hi = v.astype(jnp.bfloat16)
    lo = (v - hi.astype(jnp.float32)).astype(jnp.bfloat16)
    return hi, lo


def occupied(i, count):
    return pl.ds(i, count, stride=NO)


def prepare_kernel(*refs):
    core, got, swapped = refs[0], refs[1:5], refs[5:9]
    col_hi, col_lo, row_hi, row_lo, rows, cols = refs[9:]
    span = GROUP * NO
    count = GROUP * len(got)
    half = GROUP // 2

    def fill(row_refs, col_refs, first):
        def tile_of(k, _):
            source = pl.ds(pl.multiple_of(k * span, 8), span)
            lanes = pl.ds(pl.multiple_of(k * 128, 128), 128)
            for i in range(NO):
                for g, ref in enumerate(col_refs):
                    at = i * count + g * GROUP
                    cols[at : at + GROUP, lanes] = ref.at[source, :][occupied(i, GROUP), :]
                for g, ref in enumerate(row_refs):
                    at = i * count // 2 + g * half
                    rows[at : at + half, lanes] = ref.at[source, :][occupied(first + i, half), :]
            return 0

        lax.fori_loop(0, TILES, tile_of, 0)

    @pl.when(core[0, 0] == 0)
    def _():
        fill(got, swapped, 0)

    @pl.when(core[0, 0] != 0)
    def _():
        fill(swapped, got, half * NO)

    def halve(source, hi, lo):
        step = 128

        def body(i, _):
            at = pl.ds(pl.multiple_of(i * step, step), step)
            hi[at, :], lo[at, :] = split(source[at, :])
            return 0

        lax.fori_loop(0, source.shape[0] // step, body, 0)

    halve(rows, row_hi, row_lo)
    halve(cols, col_hi, col_lo)


def flat(v):
    return v.reshape(-1, v.shape[2])


def prepare(core, got, swapped):
    width = NO * GROUP * len(got)
    height = width // 2
    col = jax.ShapeDtypeStruct((width, NAUX), jnp.bfloat16)
    row = jax.ShapeDtypeStruct((height, NAUX), jnp.bfloat16)
    return pl.pallas_call(
        prepare_kernel,
        out_shape=(col, col, row, row, jax.ShapeDtypeStruct(row.shape, jnp.float32)),
        in_specs=[pl.BlockSpec(memory_space=pltpu.SMEM)] + [VMEM] * (2 * len(got)),
        out_specs=(VMEM,) * 5,
        scratch_shapes=[pltpu.VMEM((width, NAUX), jnp.float32)],
        compiler_params=pltpu.CompilerParams(vmem_limit_bytes=8 << 20),
        name="prepare",
    )(core, *map(flat, got), *map(flat, swapped))


def swap_chunks(v):
    lane = lax.broadcasted_iota(jnp.int32, v[0].shape, 1)
    low = lane < 64
    even = (lane // 32) % 2 == 0

    def halves(a, b):
        r = pltpu.roll(jnp.where(low, b, a), 64, 1)
        return jnp.where(low, a, r), jnp.where(low, r, b)

    def quarters(a, b):
        m = jnp.where(even, b, a)
        return (
            jnp.where(even, a, pltpu.roll(m, 32, 1)),
            jnp.where(even, pltpu.roll(m, 96, 1), b),
        )

    a0, a2 = halves(v[0], v[2])
    a1, a3 = halves(v[1], v[3])
    w0, w1 = quarters(a0, a1)
    w2, w3 = quarters(a2, a3)
    return w0, w1, w2, w3


def tile_kernel(count, scale, *refs):
    fhi, flo, chi, clo = refs[:2], refs[2:4], refs[4:6], refs[6:8]
    rhi, rlo, c_rows, row_pair = (refs[8 + k * count : 8 + (k + 1) * count] for k in range(4))
    col_pair = refs[8 + 4 * count]
    outs = refs[9 + 4 * count : 9 + 6 * count]
    energy, rows, direct, *slots = refs[9 + 6 * count :]
    na = 8
    block = NO * na
    width = direct.shape[1]
    nb = width // NO
    per = 128 // nb
    blocks = NO // per
    tall = per * na

    def span(start, size):
        if isinstance(start, int):
            return slice(start, start + size)
        return pl.ds(pl.multiple_of(start, size), size)

    def chunk(pair, n):
        piece = nb // len(pair)
        first = n * (CHUNK // nb)
        return jnp.concatenate(
            [r[span((first + i) * piece, piece), :] for i in range(CHUNK // nb) for r in pair], 0
        )

    def product(n, _):
        hi, lo = chunk(fhi, n), chunk(flo, n)
        for g in range(count):
            acc = lax.dot_general(rhi[g][...], hi, NT, preferred_element_type=jnp.float32)
            acc += lax.dot_general(rhi[g][...], lo, NT, preferred_element_type=jnp.float32)
            acc += lax.dot_general(rlo[g][...], hi, NT, preferred_element_type=jnp.float32)
            direct[g * block : (g + 1) * block, span(n * CHUNK, CHUNK)] = acc
        return 0

    chunks = width // CHUNK
    if LOOP_PRODUCT[count - 1]:
        lax.fori_loop(0, chunks, product, 0)
    else:
        for n in range(chunks):
            product(n, 0)

    def amplitudes(n, slot):
        hi, lo = slots[2 * slot], slots[2 * slot + 1]
        for jj in range(CHUNK // 128):
            j = n * (CHUNK // 128) + jj
            lanes = span(j * 128, 128)
            at = slice(jj * 128, (jj + 1) * 128)
            for g in range(count):
                top = g * block
                for i in range(blocks):
                    here = slice(top + i * tall, top + (i + 1) * tall)
                    other = direct[span(top + j * tall, tall), i * 128 : (i + 1) * 128]
                    parts = [other[k * na : (k + 1) * na] for k in range(per)]
                    value = direct[here, lanes]
                    value = value + value - jnp.concatenate(swap_chunks(parts), 0)
                    e_sum = row_pair[g][i * tall : (i + 1) * tall, :] + col_pair[0:1, lanes]
                    hi[here, at], lo[here, at] = split(value / e_sum)

    def contract(n, slot):
        hi, lo = slots[2 * slot], slots[2 * slot + 1]
        right = chunk(chi, n)
        acc = jnp.dot(hi[...], right, preferred_element_type=jnp.float32)
        acc += jnp.dot(hi[...], chunk(clo, n), preferred_element_type=jnp.float32)
        acc += jnp.dot(lo[...], right, preferred_element_type=jnp.float32)
        rows[...] += acc

    def two_chunks(m, _):
        amplitudes(2 * m + 1, 1)
        contract(2 * m, 0)
        amplitudes(2 * m + 2, 0)
        contract(2 * m + 1, 1)
        return 0

    last = chunks - 1
    rows[...] = jnp.zeros_like(rows)
    amplitudes(0, 0)
    for m in range(last // 2):
        two_chunks(m, 0)
    amplitudes(last, 1)
    contract(last - 1, 0)
    contract(last, 1)

    def finish(k, total):
        target = pl.ds(pl.multiple_of(k * GROUP * NO, 8), GROUP * NO)
        lanes = pl.ds(pl.multiple_of(k * 128, 128), 128)
        for i in range(count * NO):
            w = rows[i * na : (i + 1) * na, lanes] * scale
            g, o = i // NO, i % NO
            for h in range(2):
                out = outs[g * 2 + h].at[target, :]
                out[occupied(o, GROUP), :] = w[h * GROUP : (h + 1) * GROUP]
            total += w * c_rows[g][o * na : (o + 1) * na, lanes]
        return total

    total = lax.fori_loop(0, TILES, finish, jnp.zeros((na, 128), jnp.float32))
    energy[...] = jnp.full(energy.shape, jnp.sum(total), jnp.float32)


def tile(groups, factor, chol, row_pair, col_pair, total):
    count = len(groups)
    height = 8 * NO * count
    width = 2 * factor[0][0].shape[0]
    part = jax.ShapeDtypeStruct((TILES * NO * GROUP, 128), jnp.float32)
    out = pl.pallas_call(
        functools.partial(tile_kernel, count, -1.0 / total),
        out_shape=(part,) * (2 * count) + (jax.ShapeDtypeStruct((8, 128), jnp.float32),),
        in_specs=[VMEM] * (9 + 4 * count),
        out_specs=(VMEM,) * (2 * count + 1),
        scratch_shapes=[
            pltpu.VMEM((height, NAUX), jnp.float32),
            pltpu.VMEM((height, width), jnp.float32),
        ]
        + [pltpu.VMEM((height, CHUNK), jnp.bfloat16)] * 4,
        compiler_params=pltpu.CompilerParams(vmem_limit_bytes=(8 if count == 1 else 14) << 20),
        name="amplitude_tile",
    )(
        *[f[0] for f in factor], *[f[1] for f in factor],
        *[c[0] for c in chol], *[c[1] for c in chol],
        *[factor[g][2] for g in groups], *[factor[g][3] for g in groups],
        *[chol[g][4] for g in groups], *[row_pair[g] for g in groups], col_pair,
    )
    return [v.reshape(TILES, -1, 128) for v in out[: 2 * count]], out[2 * count]


def shards(chol, eps_occ, eps_vir):
    zh, x, c, zl, y = (lax.axis_index(a) for a in AXES)
    total = eps_vir.shape[0] * eps_occ.shape[0]

    def virtuals(places):
        ids = jnp.stack([place(*p) for p in places])
        return eps_vir.reshape(-1, 2)[ids].reshape(-1)

    order = ((0, 0), (1, 0), (0, 3), (0, 1), (0, 2), (1, 2), (1, 3), (1, 1))
    col_vir = virtuals(
        [(zh ^ f, x + d, cc, zl ^ f, y) for f, d in order for cc in (1, 0)]
    )
    row_vir = virtuals([(zh, x, c, zl ^ f, y + d) for f, d in order]).reshape(2, -1)
    col_pair = jnp.broadcast_to((col_vir[None, :] - eps_occ[:, None]).reshape(1, -1), (8, col_vir.shape[0] * NO))
    row_pair = (row_vir[:, None, :] - eps_occ[None, :, None]).reshape(2, -1, 1)
    row_pair = jnp.broadcast_to(row_pair, row_pair.shape[:2] + (128,))

    half = chol.shape[0]
    chol = jnp.transpose(chol.reshape(half, TILES, 128), (1, 0, 2))
    core = c.astype(jnp.int32).reshape(1, 1)
    chol_parts = None
    factor = chol
    energies = []
    for step in range(ITERS):
        factor_parts = gather(factor, core)
        if step == 0:
            chol_parts = factor_parts
        if step < ITERS - 1:
            (p_far, p_far_sides), e_far = tile((1,), factor_parts, chol_parts, row_pair, col_pair, total)
            (p_mine, p_sides), e_near = tile((0,), factor_parts, chol_parts, row_pair, col_pair, total)
            energies.append(e_far + e_near)
        else:
            (p_mine, p_sides, p_far, p_far_sides), e_all = tile(
                (0, 1), factor_parts, chol_parts, row_pair, col_pair, total
            )
            energies.append(e_all)
        p_mine = p_mine + y_step(p_far, 2, False)
        p_sides = p_sides + y_step(p_far_sides, 0, True)
        to_left, to_right, to_partner = p_sides[:, :half], p_sides[:, half:], p_mine[:, half:]
        if step == ITERS - 1:
            lane = lax.broadcasted_iota(jnp.int32, (8, 128), 1)
            e = jnp.where(lane == 0, energies[0], energies[1])
            e = e + hop(e, 0, 1, 0, 0) + hop(e, 0, 3, 0, 0) + hop(e, 0, 2, 0, 0)
            e = e + hop(e, 1, 0, 1, 0) + hop(e, 0, 0, 1, 2) + hop(e, 1, 0, 0, 2)
            tail = jnp.broadcast_to(e[None], (TILES, 8, 128))
            to_left, to_right, to_partner = (
                jnp.concatenate((v, tail), 1) for v in (to_left, to_right, to_partner)
            )
        a = y_step(to_left, -1, False)
        b = y_step(to_right, 1, False)
        p = y_step(to_partner, 0, True)
        work = p_mine[:, :half] + a[:, :half] + b[:, :half] + p[:, :half]
        factor = chol + work

    e = e + a[0, half:] + b[0, half:] + p[0, half:]
    e = e + core_swap(e)
    work = jnp.transpose(work, (1, 0, 2)).reshape(half, -1)
    return (work, e[0, :2] / jnp.float32(total))


def solution(mesh):
    torus = Mesh(mesh.devices.reshape(2, 4, 2, 2, 4), AXES)
    placed = (P(AXES, None), P(), P())
    return jax.shard_map(
        shards, mesh=torus, in_specs=placed, out_specs=(P(AXES, None), P()), check_vma=False
    )
```
